512 devices in a mesh: head: 16 (over z), ctx: 32 (over x, y, core).
Axes of the slice: x: 4, y: 4, z: 16, core: 2. Of those that a mesh axis runs over, the one named last changes fastest.
Arguments:
- queries: bfloat16 [2, 8192, 4096], P(None, 'ctx', 'head'), may hold values from -6 to 6
- key_vectors: bfloat16 [2, 8192, 4096], P(None, 'ctx', 'head'), may hold values from -6 to 6
- value_vectors: bfloat16 [2, 8192, 4096], P(None, 'ctx', 'head'), may hold values from -6 to 6
- gate_weight: bfloat16 [16, 256, 512], P('head'), may hold values from -0.375 to 0.375
- up_weight: bfloat16 [16, 256, 512], P('head'), may hold values from -0.375 to 0.375
- down_weight: bfloat16 [16, 256, 512], P('head'), may hold values from -0.25 to 0.25
- learn_rates: float32 [16], P('head'), may hold values from 0.2 to 1
Outputs:
- outputs: bfloat16 [2, 8192, 4096], P(None, ('ctx', 'head'))
The draws below stay inside these ranges and needn't reach their ends.
All inputs are finite; a program needn't handle non-finite values.
Results may differ from the reference program's by a relative error of at most 0.018.
Values may be sent and summed in bfloat16 or wider, within the bound.
A program may use at most 64 MiB of HBM per device.

```python
import math
import jax
import jax.numpy as jnp
from jax import lax

HEADS = 16
DH = 256
FH = 512
BLOCKS = 2
NS_ITERS = 3
BLOCK_TOK = 8192


def shard_levels(rng, dims, shards, low, high):
    level, own = 1.0, jax.random.fold_in(rng, 6)
    for axis_at, shards_of in shards:
        heights = jnp.exp(jax.random.uniform(jax.random.fold_in(own, axis_at), (shards_of,), jnp.float32, low / len(shards), high / len(shards)))
        level = level * jnp.repeat(heights, dims[axis_at] // shards_of).reshape([-1 if axis == axis_at else 1 for axis in range(len(dims))])
    return level


def bell_draw(rng, shape, width, reach, split=(), held_as=jnp.bfloat16):
    entries = width * jax.random.normal(rng, shape, jnp.float32)
    if split:
        entries = entries * shard_levels(rng, shape, split, -0.22, 0.18)
    return jnp.clip(entries, -reach, reach).astype(held_as)


def setup_inputs(seed: int = 0) -> dict:
    keys = jax.random.split(jax.random.key(seed), 8)
    return {
        "queries": bell_draw(keys[0], (BLOCKS, BLOCK_TOK, HEADS * DH), 1.0, 6.0, ((1, 32), (2, 16))),
        "key_vectors": bell_draw(keys[1], (BLOCKS, BLOCK_TOK, HEADS * DH), 1.0, 6.0, ((1, 32), (2, 16))),
        "value_vectors": bell_draw(keys[2], (BLOCKS, BLOCK_TOK, HEADS * DH), 1.0, 6.0, ((1, 32), (2, 16))),
        "gate_weight": bell_draw(keys[3], (HEADS, DH, FH), DH ** -0.5, 0.375, ((0, 16),)),
        "up_weight": bell_draw(keys[4], (HEADS, DH, FH), DH ** -0.5, 0.375, ((0, 16),)),
        "down_weight": bell_draw(keys[5], (HEADS, DH, FH), FH ** -0.5, 0.25, ((0, 16),)),
        "learn_rates": jnp.clip(jnp.exp(math.log(1.0) - 1.609438 * jax.random.uniform(keys[6], (HEADS,), jnp.float32) ** shard_levels(keys[6], (HEADS,), ((0, 16),), -0.2, 0.2)), 0.2, 1.0),
    }


COEF_A = 3.4445
COEF_B = -4.775
COEF_C = 2.0315
EPSILON = 1e-06

def forward_parts(rows, gate_w, up_w):
    rows_f = rows.astype(jnp.float32)
    pre_gate = jnp.einsum('htd,hdf->htf', rows_f, gate_w.astype(jnp.float32))
    pre_up = jnp.einsum('htd,hdf->htf', rows_f, up_w.astype(jnp.float32))
    return (pre_gate, pre_up)

def orthogonalize(gradient):
    magnitude = jnp.sqrt(lax.optimization_barrier(jnp.sum(gradient * gradient, axis=(1, 2))))
    iterate = gradient / (magnitude + EPSILON)[:, None, None]
    for turn_index in range(NS_ITERS):
        gram_matrix = jnp.einsum('hdf,hef->hde', iterate, iterate, precision=lax.Precision.HIGHEST)
        polynomial = COEF_B * gram_matrix + COEF_C * jnp.einsum('hde,hef->hdf', gram_matrix, gram_matrix, precision=lax.Precision.HIGHEST)
        iterate = COEF_A * iterate + jnp.einsum('hde,hef->hdf', polynomial, iterate, precision=lax.Precision.HIGHEST)
    return iterate

def by_heads(block_rows):
    return block_rows.reshape(block_rows.shape[0], HEADS, DH).transpose(1, 0, 2)

def reference(queries, key_vectors, value_vectors, gate_weight, up_weight, down_weight, learn_rates):
    weights_f = [gate_weight.astype(jnp.float32), up_weight.astype(jnp.float32), down_weight.astype(jnp.float32)]
    weights_b = [gate_weight, up_weight, down_weight]
    results = []
    for block_index in range(BLOCKS):
        keys_h = by_heads(key_vectors[block_index])
        values_h = by_heads(value_vectors[block_index])
        pre_gate, pre_up = forward_parts(keys_h, weights_b[0], weights_b[1])
        sigmoid_g = jax.nn.sigmoid(pre_gate)
        activated = pre_gate * sigmoid_g
        gated = (activated * pre_up).astype(jnp.bfloat16)
        values_f = values_h.astype(jnp.float32)
        back = -jnp.einsum('htd,hdf->htf', values_f, weights_b[2].astype(jnp.float32))
        d_up = (back * activated).astype(jnp.bfloat16)
        d_gate = (back * pre_up * sigmoid_g * (1.0 + pre_gate * (1.0 - sigmoid_g))).astype(jnp.bfloat16)
        keys_f = keys_h.astype(jnp.float32)
        grad_gate = jnp.einsum('htd,htf->hdf', keys_f, d_gate.astype(jnp.float32))
        grad_up = jnp.einsum('htd,htf->hdf', keys_f, d_up.astype(jnp.float32))
        grad_down = -jnp.einsum('htd,htf->hdf', values_f, gated.astype(jnp.float32))
        grads = [grad_gate, grad_up, grad_down]
        for which in range(3):
            weights_f[which] = weights_f[which] - learn_rates[:, None, None] * orthogonalize(grads[which])
            weights_b[which] = weights_f[which].astype(jnp.bfloat16)
        queries_h = by_heads(queries[block_index])
        q_gate, q_up = forward_parts(queries_h, weights_b[0], weights_b[1])
        q_gated = (jax.nn.silu(q_gate) * q_up).astype(jnp.bfloat16)
        block_out = jnp.einsum('htf,hdf->htd', q_gated.astype(jnp.float32), weights_b[2].astype(jnp.float32))
        results.append(block_out.transpose(1, 0, 2).reshape(block_out.shape[1], HEADS * DH).astype(jnp.bfloat16))
    return jnp.stack(results)
```

```python
import jax
import jax.numpy as jnp
from jax import lax
from jax.experimental import pallas as pl
from jax.experimental.pallas import tpu as pltpu
from jax.sharding import PartitionSpec as P

BLOCKS = 2
NS_ITERS = 3
COEF_A = 3.4445
COEF_B = -4.775
COEF_C = 2.0315
EPSILON = 1e-06

SIDE = 4
CHIPS = SIDE * SIDE
HEADS = 16
DH = 256
FH = 512
HALF = 256
OWN = DH // CHIPS
MESH = pl.DeviceIdType.MESH

STEPS = sorted(
    [(dx, dy) for dx in range(SIDE) for dy in range(SIDE) if (dx, dy) != (0, 0)],
    key=lambda s: -(min(s[0], SIDE - s[0]) + min(s[1], SIDE - s[1])),
)
HOPS = sorted(range(1, HEADS), key=lambda o: -min(o, HEADS - o))


def nn(a, b):
    return jnp.dot(a, b, preferred_element_type=jnp.float32)


def nt(a, b):
    return lax.dot_general(a, b, (((1,), (1,)), ((), ())), preferred_element_type=jnp.float32)


def kernel(
    lr_ref,
    q_ref,
    k_ref,
    v_ref,
    wg_ref,
    wu_ref,
    wd_ref,
    out_ref,
    mine,
    theirs,
    pairs,
    shares,
    whole,
    master,
    fast,
    iterate,
    made,
    pair_s,
    pair_r,
    share_s,
    share_r,
    whole_s,
    whole_r,
    twin_s,
    twin_r,
    out_s,
    out_r,
):
    bf16, f32 = jnp.bfloat16, jnp.float32
    head = lax.axis_index("head")
    ctx = lax.axis_index("ctx")
    core = ctx % 2
    chip = ctx // 2
    x, y = chip // SIDE, chip % SIDE
    twin = {"ctx": ctx + 1 - 2 * core}

    def to_chip(step, sign=1):
        return (x + sign * step[0] + SIDE) % SIDE * SIDE + (y + sign * step[1] + SIDE) % SIDE

    def on_chip(other):
        return {"ctx": other * 2 + core}

    def send(src, dst, s, r, device):
        return pltpu.make_async_remote_copy(
            src_ref=src,
            dst_ref=dst,
            send_sem=s,
            recv_sem=r,
            device_id=device,
            device_id_type=MESH,
        )

    barrier = pltpu.get_barrier_semaphore()
    for o in HOPS:
        pl.semaphore_signal(
            barrier, inc=1, device_id={"head": (head + o) % HEADS}, device_id_type=MESH
        )
    for step in STEPS:
        pl.semaphore_signal(
            barrier, inc=1, device_id=on_chip(to_chip(step)), device_id_type=MESH
        )
    pl.semaphore_signal(barrier, inc=1, device_id=twin, device_id_type=MESH)

    master[0] = wg_ref[0].astype(f32)
    master[1] = wu_ref[0].astype(f32)
    master[2] = wd_ref[0].astype(f32)
    fast[0] = wg_ref[0]
    fast[1] = wu_ref[0]
    fast[2] = wd_ref[0]

    def pair_copy(b, m):
        return send(
            mine.at[b, 1 - core, m], theirs.at[b, m], pair_s.at[b, m], pair_r.at[b, m], twin
        )

    def share_copy(b, i):
        other = to_chip(STEPS[i])
        return send(
            pairs.at[b, other], shares.at[b, i], share_s.at[b, i], share_r.at[b, i], on_chip(other)
        )

    def whole_copy(b, i):
        here = whole.at[b, core, chip]
        return send(
            here, here, whole_s.at[b, i], whole_r.at[b, i], on_chip(to_chip(STEPS[i]))
        )

    def twin_copy(b, i):
        slot = chip if i == len(STEPS) else to_chip(STEPS[i], -1)
        here = whole.at[b, core, slot]
        return send(here, here, twin_s.at[b, i], twin_r.at[b, i], twin)

    def out_copy(b, i):
        other = (head + HOPS[i]) % HEADS
        columns = pl.ds(pl.multiple_of(head * DH, DH), DH)
        return send(
            made.at[b, other],
            out_ref.at[b, :, columns],
            out_s.at[b, i],
            out_r.at[b, i],
            {"head": other},
        )

    def gradients(b):
        keys, values = k_ref[b], v_ref[b]
        gate = nn(keys, fast[0])
        up = nn(keys, fast[1])
        sig = jax.nn.sigmoid(gate)
        act = gate * sig
        gated = (act * up).astype(bf16)
        values_t = values.T
        for j in range(2):
            mine[b, j, 2] = nn(values_t, gated[:, j * HALF : (j + 1) * HALF]).astype(bf16)
        back = nn(values, fast[2])
        d_up = (back * act).astype(bf16)
        d_gate = (back * up * sig * (1.0 + gate * (1.0 - sig))).astype(bf16)
        keys_t = keys.T
        for m, d in ((0, d_gate), (1, d_up)):
            for j in range(2):
                mine[b, j, m] = nn(keys_t, d[:, j * HALF : (j + 1) * HALF]).astype(bf16)

    def start_pair(b):
        for m in (2, 0, 1):
            pair_copy(b, m).start()

    def start_shares(b):
        for m in (2, 0, 1):
            pair_copy(b, m).wait_recv()
            both = mine[b, core, m].astype(f32) + theirs[b, m].astype(f32)
            pairs[b, :, m] = both.astype(bf16).reshape(CHIPS, OWN, HALF)
        for i in range(len(STEPS)):
            share_copy(b, i).start()

    def finish_shares(b):
        total = pairs[b, chip].astype(f32)
        for i in range(len(STEPS)):
            share_copy(b, i).wait_recv()
            total = total + shares[b, i].astype(f32)
        whole[b, core, chip] = total.astype(bf16)
        for i in range(len(STEPS)):
            whole_copy(b, i).start()
        twin_copy(b, len(STEPS)).start()
        for i in range(len(STEPS)):
            whole_copy(b, i).wait_recv()
            twin_copy(b, i).start()
        for i in range(len(STEPS) + 1):
            twin_copy(b, i).wait_recv()

    def update(b):
        for m in range(3):
            grad = jnp.concatenate(
                [whole[b, j, :, m].reshape(DH, HALF) for j in range(2)], axis=1
            )
            grad_f = grad.astype(f32)
            inv = 1.0 / (jnp.sqrt(jnp.sum(grad_f * grad_f, keepdims=True)) + EPSILON)
            gram = nt(grad, grad) * inv * inv
            gram_b = gram.astype(bf16)
            poly = COEF_B * gram + COEF_C * nn(gram_b, gram_b)
            iterate[m] = (COEF_A * grad_f + nn(poly.astype(bf16), grad)) * inv
        for turn in range(1, NS_ITERS):
            for m in range(3):
                now = iterate[m]
                now_b = now.astype(bf16)
                gram = nt(now_b, now_b)
                gram_b = gram.astype(bf16)
                poly = COEF_B * gram + COEF_C * nn(gram_b, gram_b)
                iterate[m] = COEF_A * now + nn(poly.astype(bf16), now_b)
        for m in range(3):
            moved = master[m] + lr_ref[0] * iterate[m]
            master[m] = moved
            fast[m] = moved.astype(bf16)

    def answer(b):
        rows = q_ref[b]
        gate = nn(rows, fast[0])
        up = nn(rows, fast[1])
        gated = (gate * jax.nn.sigmoid(gate) * up).astype(bf16)
        made[b] = nt(gated, fast[2]).astype(bf16).reshape(HEADS, OWN, DH)
        for i in range(len(HOPS)):
            out_copy(b, i).start()
        columns = pl.ds(pl.multiple_of(head * DH, DH), DH)
        out_ref[b, :, columns] = made[b, head]

    gradients(0)
    pl.semaphore_wait(barrier, len(HOPS) + len(STEPS) + 1)
    start_pair(0)
    start_shares(0)
    finish_shares(0)
    update(0)
    gradients(1)
    start_pair(1)
    start_shares(1)
    answer(0)
    finish_shares(1)
    update(1)
    answer(1)
    for b in range(BLOCKS):
        for m in range(3):
            pair_copy(b, m).wait_send()
        for i in range(len(STEPS)):
            share_copy(b, i).wait_send()
            whole_copy(b, i).wait_send()
        for i in range(len(STEPS) + 1):
            twin_copy(b, i).wait_send()
        for i in range(len(HOPS)):
            out_copy(b, i).wait()


def on_device(queries, key_vectors, value_vectors, gate_weight, up_weight, down_weight, learn_rates):
    bf16, f32 = jnp.bfloat16, jnp.float32
    others, hops = len(STEPS), len(HOPS)
    vmem = pl.BlockSpec(memory_space=pltpu.VMEM)
    dma = pltpu.SemaphoreType.DMA
    return pl.pallas_call(
        kernel,
        out_shape=jax.ShapeDtypeStruct((BLOCKS, OWN, HEADS * DH), bf16),
        in_specs=[pl.BlockSpec(memory_space=pltpu.SMEM)] + [vmem] * 6,
        out_specs=vmem,
        scratch_shapes=[
            pltpu.VMEM((BLOCKS, 2, 3, DH, HALF), bf16),
            pltpu.VMEM((BLOCKS, 3, DH, HALF), bf16),
            pltpu.VMEM((BLOCKS, CHIPS, 3, OWN, HALF), bf16),
            pltpu.VMEM((BLOCKS, others, 3, OWN, HALF), bf16),
            pltpu.VMEM((BLOCKS, 2, CHIPS, 3, OWN, HALF), bf16),
            pltpu.VMEM((3, DH, FH), f32),
            pltpu.VMEM((3, DH, FH), bf16),
            pltpu.VMEM((3, DH, FH), f32),
            pltpu.VMEM((BLOCKS, HEADS, OWN, DH), bf16),
            dma((BLOCKS, 3)),
            dma((BLOCKS, 3)),
            dma((BLOCKS, others)),
            dma((BLOCKS, others)),
            dma((BLOCKS, others)),
            dma((BLOCKS, others)),
            dma((BLOCKS, others + 1)),
            dma((BLOCKS, others + 1)),
            dma((BLOCKS, hops)),
            dma((BLOCKS, hops)),
        ],
        compiler_params=pltpu.CompilerParams(
            collective_id=0, has_side_effects=True, vmem_limit_bytes=48 * 1024 * 1024
        ),
        name="ttt",
    )(learn_rates, queries, key_vectors, value_vectors, gate_weight, up_weight, down_weight)


def solution(mesh):
    return jax.shard_map(
        on_device,
        mesh=mesh,
        in_specs=(
            P(None, "ctx", "head"),
            P(None, "ctx", "head"),
            P(None, "ctx", "head"),
            P("head", None, None),
            P("head", None, None),
            P("head", None, None),
            P("head"),
        ),
        out_specs=P(None, ("ctx", "head"), None),
        check_vma=False,
    )
```

```python
import jax
import jax.numpy as jnp
from jax import lax
from jax.experimental import pallas as pl
from jax.experimental.pallas import tpu as pltpu
from jax.sharding import PartitionSpec as P

BLOCKS = 2
NS_ITERS = 3
COEF_A = 3.4445
COEF_B = -4.775
COEF_C = 2.0315
EPSILON = 1e-06

SIDE = 4
CHIPS = SIDE * SIDE
HEADS = 16
DH = 256
FH = 512
HALF = 256
OWN = DH // CHIPS
MESH = pl.DeviceIdType.MESH

STEPS = sorted(
    [(dx, dy) for dx in range(SIDE) for dy in range(SIDE) if (dx, dy) != (0, 0)],
    key=lambda s: -(min(s[0], SIDE - s[0]) + min(s[1], SIDE - s[1])),
)
RING = (1, 2, 4)
HOPS = sorted(range(1, HEADS), key=lambda o: -min(o, HEADS - o))


def nn(a, b):
    return jnp.dot(a, b, preferred_element_type=jnp.float32)


def nt(a, b):
    return lax.dot_general(a, b, (((1,), (1,)), ((), ())), preferred_element_type=jnp.float32)


def kernel(
    lr_ref,
    q_hbm,
    k_hbm,
    v_hbm,
    wg_hbm,
    wu_hbm,
    wd_hbm,
    out_ref,
    q_ref,
    k_ref,
    v_ref,
    mine,
    theirs,
    pairs,
    shares,
    whole,
    master,
    fast,
    made,
    load_s,
    pair_s,
    pair_r,
    share_s,
    share_r,
    whole_s,
    whole_r,
    twin_s,
    twin_r,
    out_s,
    out_r,
    ring,
):
    bf16, f32 = jnp.bfloat16, jnp.float32
    head = lax.axis_index("head")
    ctx = lax.axis_index("ctx")
    core = ctx % 2
    chip = ctx // 2
    x, y = chip // SIDE, chip % SIDE
    twin = {"ctx": ctx + 1 - 2 * core}

    def to_chip(step, sign=1):
        return (x + sign * step[0] + SIDE) % SIDE * SIDE + (y + sign * step[1] + SIDE) % SIDE

    def on_chip(other):
        return {"ctx": other * 2 + core}

    def send(src, dst, s, r, device):
        return pltpu.make_async_remote_copy(
            src_ref=src,
            dst_ref=dst,
            send_sem=s,
            recv_sem=r,
            device_id=device,
            device_id_type=MESH,
        )

    barrier = pltpu.get_barrier_semaphore()
    for z in (1, HEADS - 1):
        pl.semaphore_signal(
            barrier, inc=1, device_id={"head": (head + z) % HEADS}, device_id_type=MESH
        )
    for step in STEPS:
        pl.semaphore_signal(
            barrier, inc=1, device_id=on_chip(to_chip(step)), device_id_type=MESH
        )
    pl.semaphore_signal(barrier, inc=1, device_id=twin, device_id_type=MESH)

    loads = [
        pltpu.make_async_copy(src, dst, load_s.at[i])
        for i, (src, dst) in enumerate(
            (
                (k_hbm, k_ref),
                (wg_hbm.at[0], fast.at[0]),
                (wu_hbm.at[0], fast.at[1]),
                (v_hbm, v_ref),
                (wd_hbm.at[0], fast.at[2]),
                (q_hbm, q_ref),
            )
        )
    ]
    for load in loads:
        load.start()

    def ring_signal(level):
        for z in (RING[level], HEADS - RING[level]):
            pl.semaphore_signal(
                ring.at[level], inc=1, device_id={"head": (head + z) % HEADS}, device_id_type=MESH
            )

    def ring_wait(level):
        pl.semaphore_wait(ring.at[level], 2)

    def pair_copy(b, m):
        return send(
            mine.at[b, 1 - core, m], theirs.at[b, m], pair_s.at[b, m], pair_r.at[b, m], twin
        )

    def share_copy(b, i):
        other = to_chip(STEPS[i])
        return send(
            pairs.at[b, other], shares.at[b, i], share_s.at[b, i], share_r.at[b, i], on_chip(other)
        )

    def whole_copy(b, i):
        here = whole.at[b, core, chip]
        return send(
            here, here, whole_s.at[b, i], whole_r.at[b, i], on_chip(to_chip(STEPS[i]))
        )

    def twin_copy(b, i):
        slot = chip if i == len(STEPS) else to_chip(STEPS[i], -1)
        here = whole.at[b, core, slot]
        return send(here, here, twin_s.at[b, i], twin_r.at[b, i], twin)

    def out_copy(b, i):
        other = (head + HOPS[i]) % HEADS
        columns = pl.ds(pl.multiple_of(head * DH, DH), DH)
        return send(
            made.at[b, other],
            out_ref.at[b, :, columns],
            out_s.at[b, i],
            out_r.at[b, i],
            {"head": other},
        )

    def gradients(b):
        if b == 0:
            for load in loads[:3]:
                load.wait()
        keys = k_ref[b]
        gate = nn(keys, fast[0])
        up = nn(keys, fast[1])
        sig = jax.nn.sigmoid(gate)
        act = gate * sig
        gated = (act * up).astype(bf16)
        if b == 0:
            for load in loads[3:5]:
                load.wait()
        values = v_ref[b]
        values_t = values.T
        for j in range(2):
            mine[b, j, 2] = nn(values_t, gated[:, j * HALF : (j + 1) * HALF]).astype(bf16)
        back = nn(values, fast[2])
        d_up = (back * act).astype(bf16)
        d_gate = (back * up * sig * (1.0 + gate * (1.0 - sig))).astype(bf16)
        keys_t = keys.T
        for m, d in ((0, d_gate), (1, d_up)):
            for j in range(2):
                mine[b, j, m] = nn(keys_t, d[:, j * HALF : (j + 1) * HALF]).astype(bf16)

    def start_pair(b):
        for m in (2, 0, 1):
            pair_copy(b, m).start()

    def start_shares(b):
        for m in (2, 0, 1):
            pair_copy(b, m).wait_recv()
            both = mine[b, core, m].astype(f32) + theirs[b, m].astype(f32)
            pairs[b, :, m] = both.astype(bf16).reshape(CHIPS, OWN, HALF)
        for i in range(len(STEPS)):
            share_copy(b, i).start()

    def start_wholes(b):
        total = pairs[b, chip].astype(f32)
        for i in range(len(STEPS)):
            share_copy(b, i).wait_recv()
            total = total + shares[b, i].astype(f32)
        whole[b, core, chip] = total.astype(bf16)
        for i in range(len(STEPS)):
            whole_copy(b, i).start()
        twin_copy(b, len(STEPS)).start()

    def finish_wholes(b):
        for i in range(len(STEPS)):
            whole_copy(b, i).wait_recv()
            twin_copy(b, i).start()
        for i in range(len(STEPS) + 1):
            twin_copy(b, i).wait_recv()

    def update(b):
        grads = [
            jnp.concatenate([whole[b, j, :, m].reshape(DH, HALF) for j in range(2)], axis=1)
            for m in range(3)
        ]
        now = [g.astype(f32) for g in grads]
        sizes = [jnp.sum(g * g, keepdims=True) for g in now]
        scales = [1.0 / (jnp.sqrt(size) + EPSILON) for size in sizes]
        now_b = grads
        for turn in range(NS_ITERS):
            grams = [nt(g, g) for g in now_b]
            if turn == 0:
                grams = [g * s * s for g, s in zip(grams, scales)]
            grams_b = [g.astype(bf16) for g in grams]
            polys = [COEF_B * g + COEF_C * nn(h, h) for g, h in zip(grams, grams_b)]
            now = [
                COEF_A * g + nn(poly.astype(bf16), h) for g, poly, h in zip(now, polys, now_b)
            ]
            if turn == 0:
                now = [g * s for g, s in zip(now, scales)]
            now_b = [g.astype(bf16) for g in now]
        for m in range(3):
            before = fast[m].astype(f32) if b == 0 else master[m]
            moved = before + lr_ref[0] * now[m]
            if b + 1 < BLOCKS:
                master[m] = moved
            fast[m] = moved.astype(bf16)

    def answer(b):
        if b == 0:
            loads[5].wait()
        rows = q_ref[b]
        gate = nn(rows, fast[0])
        up = nn(rows, fast[1])
        gated = (gate * jax.nn.sigmoid(gate) * up).astype(bf16)
        made[b] = nt(gated, fast[2]).astype(bf16).reshape(HEADS, OWN, DH)
        for i in range(len(HOPS)):
            out_copy(b, i).start()
        columns = pl.ds(pl.multiple_of(head * DH, DH), DH)
        out_ref[b, :, columns] = made[b, head]

    gradients(0)
    pl.semaphore_wait(barrier, len(STEPS) + 3)
    ring_signal(0)
    start_pair(0)
    start_shares(0)
    ring_wait(0)
    ring_signal(1)
    start_wholes(0)
    ring_wait(1)
    ring_signal(2)
    finish_wholes(0)
    update(0)
    gradients(1)
    start_pair(1)
    start_shares(1)
    ring_wait(2)
    answer(0)
    start_wholes(1)
    finish_wholes(1)
    update(1)
    answer(1)
    for b in range(BLOCKS):
        for m in range(3):
            pair_copy(b, m).wait_send()
        for i in range(len(STEPS)):
            share_copy(b, i).wait_send()
            whole_copy(b, i).wait_send()
        for i in range(len(STEPS) + 1):
            twin_copy(b, i).wait_send()
        for i in range(len(HOPS)):
            out_copy(b, i).wait()


def on_device(queries, key_vectors, value_vectors, gate_weight, up_weight, down_weight, learn_rates):
    bf16, f32 = jnp.bfloat16, jnp.float32
    others, hops = len(STEPS), len(HOPS)
    vmem = pl.BlockSpec(memory_space=pltpu.VMEM)
    hbm = pl.BlockSpec(memory_space=pltpu.HBM)
    dma = pltpu.SemaphoreType.DMA
    return pl.pallas_call(
        kernel,
        out_shape=jax.ShapeDtypeStruct((BLOCKS, OWN, HEADS * DH), bf16),
        in_specs=[pl.BlockSpec(memory_space=pltpu.SMEM)] + [hbm] * 6,
        out_specs=vmem,
        scratch_shapes=[
            pltpu.VMEM((BLOCKS, DH, DH), bf16),
            pltpu.VMEM((BLOCKS, DH, DH), bf16),
            pltpu.VMEM((BLOCKS, DH, DH), bf16),
            pltpu.VMEM((BLOCKS, 2, 3, DH, HALF), bf16),
            pltpu.VMEM((BLOCKS, 3, DH, HALF), bf16),
            pltpu.VMEM((BLOCKS, CHIPS, 3, OWN, HALF), bf16),
            pltpu.VMEM((BLOCKS, others, 3, OWN, HALF), bf16),
            pltpu.VMEM((BLOCKS, 2, CHIPS, 3, OWN, HALF), bf16),
            pltpu.VMEM((3, DH, FH), f32),
            pltpu.VMEM((3, DH, FH), bf16),
            pltpu.VMEM((BLOCKS, HEADS, OWN, DH), bf16),
            dma((6,)),
            dma((BLOCKS, 3)),
            dma((BLOCKS, 3)),
            dma((BLOCKS, others)),
            dma((BLOCKS, others)),
            dma((BLOCKS, others)),
            dma((BLOCKS, others)),
            dma((BLOCKS, others + 1)),
            dma((BLOCKS, others + 1)),
            dma((BLOCKS, hops)),
            dma((BLOCKS, hops)),
            pltpu.SemaphoreType.REGULAR((len(RING),)),
        ],
        compiler_params=pltpu.CompilerParams(
            collective_id=0, has_side_effects=True, vmem_limit_bytes=66_500_000
        ),
        name="ttt",
    )(learn_rates, queries, key_vectors, value_vectors, gate_weight, up_weight, down_weight)


def solution(mesh):
    return jax.shard_map(
        on_device,
        mesh=mesh,
        in_specs=(
            P(None, "ctx", "head"),
            P(None, "ctx", "head"),
            P(None, "ctx", "head"),
            P("head", None, None),
            P("head", None, None),
            P("head", None, None),
            P("head"),
        ),
        out_specs=P(None, ("ctx", "head"), None),
        check_vma=False,
    )
```

```python
import jax
import jax.numpy as jnp
from jax import lax
from jax.experimental import pallas as pl
from jax.experimental.pallas import tpu as pltpu
from jax.sharding import PartitionSpec as P

BLOCKS = 2
NS_ITERS = 3
COEF_A = 3.4445
COEF_B = -4.775
COEF_C = 2.0315
EPSILON = 1e-06

SIDE = 4
CHIPS = SIDE * SIDE
HEADS = 16
DH = 256
FH = 512
HALF = 256
OWN = DH // CHIPS
MESH = pl.DeviceIdType.MESH

STEPS = sorted(
    [(dx, dy) for dx in range(SIDE) for dy in range(SIDE) if (dx, dy) != (0, 0)],
    key=lambda s: -(min(s[0], SIDE - s[0]) + min(s[1], SIDE - s[1])),
)
RING = (1, 2, 4)
ORDER = (2, 1, 0)
PARTS = 2
HOPS = sorted(range(1, HEADS), key=lambda o: -min(o, HEADS - o))


def nn(a, b):
    return jnp.dot(a, b, preferred_element_type=jnp.float32)


def nt(a, b):
    return lax.dot_general(a, b, (((1,), (1,)), ((), ())), preferred_element_type=jnp.float32)


def kernel(
    lr_ref,
    q_hbm,
    k_hbm,
    v_hbm,
    wg_hbm,
    wu_hbm,
    wd_hbm,
    out_ref,
    q_ref,
    k_ref,
    v_ref,
    mine,
    theirs,
    pairs,
    shares,
    whole,
    master,
    fast,
    made,
    load_s,
    pair_s,
    pair_r,
    share_s,
    share_r,
    whole_s,
    whole_r,
    twin_s,
    twin_r,
    out_s,
    out_r,
    ring,
):
    bf16, f32 = jnp.bfloat16, jnp.float32
    head = lax.axis_index("head")
    ctx = lax.axis_index("ctx")
    core = ctx % 2
    chip = ctx // 2
    x, y = chip // SIDE, chip % SIDE
    twin = {"ctx": ctx + 1 - 2 * core}

    def to_chip(step, sign=1):
        return (x + sign * step[0] + SIDE) % SIDE * SIDE + (y + sign * step[1] + SIDE) % SIDE

    def on_chip(other):
        return {"ctx": other * 2 + core}

    def send(src, dst, s, r, device):
        return pltpu.make_async_remote_copy(
            src_ref=src,
            dst_ref=dst,
            send_sem=s,
            recv_sem=r,
            device_id=device,
            device_id_type=MESH,
        )

    def load(i, src, dst):
        return pltpu.make_async_copy(src, dst, load_s.at[i])

    first = [
        load(0, k_hbm.at[0], k_ref.at[0]),
        load(1, wg_hbm.at[0], fast.at[0]),
        load(2, wu_hbm.at[0], fast.at[1]),
        load(3, v_hbm.at[0], v_ref.at[0]),
        load(4, wd_hbm.at[0], fast.at[2]),
    ]
    second = [load(5, k_hbm.at[1], k_ref.at[1]), load(6, v_hbm.at[1], v_ref.at[1])]
    for copy in first:
        copy.start()

    barrier = pltpu.get_barrier_semaphore()
    for z in (1, HEADS - 1):
        pl.semaphore_signal(
            barrier, inc=1, device_id={"head": (head + z) % HEADS}, device_id_type=MESH
        )
    for step in STEPS:
        pl.semaphore_signal(
            barrier, inc=1, device_id=on_chip(to_chip(step)), device_id_type=MESH
        )
    pl.semaphore_signal(barrier, inc=1, device_id=twin, device_id_type=MESH)

    def ring_signal(level):
        for z in (RING[level], HEADS - RING[level]):
            pl.semaphore_signal(
                ring.at[level], inc=1, device_id={"head": (head + z) % HEADS}, device_id_type=MESH
            )

    def ring_wait(level):
        pl.semaphore_wait(ring.at[level], 2)

    def load_queries():
        for b in range(BLOCKS):
            for i, o in enumerate(HOPS + [0]):
                rows = pl.ds(pl.multiple_of((head + o) % HEADS * OWN, OWN), OWN)
                load(7, q_hbm.at[b, rows], q_ref.at[b, i]).start()

    def pair_copy(b, m):
        return send(
            mine.at[b, 1 - core, m], theirs.at[b, m], pair_s.at[b, m], pair_r.at[b, m], twin
        )

    def share_copy(b, m, i):
        other = to_chip(STEPS[i])
        return send(
            pairs.at[b, m, other],
            shares.at[b, m, i],
            share_s.at[b, m],
            share_r.at[b, m],
            on_chip(other),
        )

    def all_shares(b, m):
        block = shares.at[b, m]
        return send(block, block, share_s.at[b, m], share_r.at[b, m], twin)

    def whole_copy(b, m, i):
        here = whole.at[b, m, core, chip]
        return send(
            here, here, whole_s.at[b, m], whole_r.at[b, m, i], on_chip(to_chip(STEPS[i]))
        )

    def all_wholes(b, m):
        block = shares.at[b, m]
        return send(block, block, whole_s.at[b, m], whole_r.at[b, m, 0], twin)

    def twin_copy(b, m, slot):
        here = whole.at[b, m, core, slot]
        return send(here, here, twin_s.at[b, m], twin_r.at[b, m], twin)

    def all_twins(b, m):
        block = whole.at[b, m, 1 - core]
        return send(block, block, twin_s.at[b, m], twin_r.at[b, m], twin)

    columns = pl.ds(pl.multiple_of(head * DH, DH), DH)

    def out_copy(b, i):
        return send(
            made.at[b, i],
            out_ref.at[b, :, columns],
            out_s.at[b],
            out_r.at[b],
            {"head": (head + HOPS[i]) % HEADS},
        )

    def all_outs(b):
        block = made.at[b, pl.ds(0, len(HOPS))]
        return send(block, block, out_s.at[b], out_r.at[b], twin)

    def gradients(b):
        def hand_over(m, rows_t, d):
            for j in range(2):
                mine[b, j, m] = nn(rows_t, d[:, j * HALF : (j + 1) * HALF]).astype(bf16)

        if b == 0:
            for copy in first[:3]:
                copy.wait()
        else:
            for copy in second:
                copy.wait()
        keys = k_ref[b]
        gate = nn(keys, fast[0])
        up = nn(keys, fast[1])
        sig = jax.nn.sigmoid(gate)
        act = gate * sig
        gated = (act * up).astype(bf16)
        if b == 0:
            for copy in first[3:]:
                copy.wait()
        values = v_ref[b]
        hand_over(2, values.T, gated)
        if b == 0:
            pl.semaphore_wait(barrier, len(STEPS) + 3)
            ring_signal(0)
        pair_copy(b, 2).start()
        back = nn(values, fast[2])
        keys_t = keys.T
        hand_over(1, keys_t, (back * act).astype(bf16))
        pair_copy(b, 1).start()
        d_gate = (back * up * sig * (1.0 + gate * (1.0 - sig))).astype(bf16)
        hand_over(0, keys_t, d_gate)
        pair_copy(b, 0).start()

    def start_shares(b):
        for m in ORDER:
            pair_copy(b, m).wait_recv()
            both = mine[b, core, m].astype(f32) + theirs[b, m].astype(f32)
            pairs[b, m] = both.astype(bf16).reshape(CHIPS, OWN, HALF)
            for i in range(len(STEPS)):
                share_copy(b, m, i).start()

    def start_wholes(b):
        for m in ORDER:
            all_shares(b, m).wait_recv()
            total = pairs[b, m, chip].astype(f32)
            for i in range(len(STEPS)):
                total = total + shares[b, m, i].astype(f32)
            whole[b, m, core, chip] = total.astype(bf16)
            for i in range(len(STEPS)):
                whole_copy(b, m, i).start()
            twin_copy(b, m, chip).start()

    def forward(b, m):
        for i in range(len(STEPS)):
            whole_copy(b, m, i).wait_recv()
            twin_copy(b, m, to_chip(STEPS[i], -1)).start()

    def finish_wholes(b):
        forward(b, 2)
        forward(b, 1)
        all_twins(b, 2).wait_recv()
        update(b, (2,))
        forward(b, 0)
        all_twins(b, 1).wait_recv()
        all_twins(b, 0).wait_recv()
        update(b, (0, 1))

    def update(b, which):
        now_b = [
            jnp.concatenate([whole[b, m, j].reshape(DH, HALF) for j in range(2)], axis=1)
            for m in which
        ]
        now = [g.astype(f32) for g in now_b]
        sizes = [jnp.sum(g * g, keepdims=True) for g in now]
        scales = [1.0 / (jnp.sqrt(size) + EPSILON) for size in sizes]
        for turn in range(NS_ITERS):
            grams = [nt(g, g) for g in now_b]
            if turn == 0:
                grams = [g * s * s for g, s in zip(grams, scales)]
            grams_b = [g.astype(bf16) for g in grams]
            polys = [COEF_B * g + COEF_C * nn(h, h) for g, h in zip(grams, grams_b)]
            now = [
                COEF_A * g + nn(poly.astype(bf16), h) for g, poly, h in zip(now, polys, now_b)
            ]
            if turn == 0:
                now = [g * s for g, s in zip(now, scales)]
            now_b = [g.astype(bf16) for g in now]
        for m, step in zip(which, now):
            before = fast[m].astype(f32) if b == 0 else master[m]
            moved = before + lr_ref[0] * step
            if b + 1 < BLOCKS:
                master[m] = moved
            fast[m] = moved.astype(bf16)

    def answer(b):
        for part in range(PARTS):
            size = HEADS // PARTS
            rows = q_ref[b, part * size : (part + 1) * size].reshape(size * OWN, DH)
            gate = nn(rows, fast[0])
            up = nn(rows, fast[1])
            gated = (gate * jax.nn.sigmoid(gate) * up).astype(bf16)
            results = nt(gated, fast[2]).astype(bf16)
            made[b, part * size : (part + 1) * size] = results.reshape(size, OWN, DH)
            for i in range(part * size, min((part + 1) * size, len(HOPS))):
                out_copy(b, i).start()
        out_ref[b, :, columns] = made[b, len(HOPS)]

    gradients(0)
    start_shares(0)
    for copy in second:
        copy.start()
    load_queries()
    ring_wait(0)
    ring_signal(1)
    start_wholes(0)
    ring_wait(1)
    ring_signal(2)
    finish_wholes(0)
    gradients(1)
    start_shares(1)
    ring_wait(2)
    load(7, q_ref, q_ref).wait()
    answer(0)
    start_wholes(1)
    finish_wholes(1)
    answer(1)
    for b in range(BLOCKS):
        for m in ORDER:
            pair_copy(b, m).wait_send()
            all_shares(b, m).wait_send()
            all_wholes(b, m).wait_send()
            all_twins(b, m).wait_send()
        all_outs(b).wait()


def on_device(*operands):
    *arrays, learn_rates = operands
    bf16, f32 = jnp.bfloat16, jnp.float32
    others = len(STEPS)
    vmem = pl.BlockSpec(memory_space=pltpu.VMEM)
    hbm = pl.BlockSpec(memory_space=pltpu.HBM)
    dma = pltpu.SemaphoreType.DMA
    return pl.pallas_call(
        kernel,
        out_shape=jax.ShapeDtypeStruct((BLOCKS, OWN, HEADS * DH), bf16),
        in_specs=[pl.BlockSpec(memory_space=pltpu.SMEM)] + [hbm] * 6,
        out_specs=vmem,
        scratch_shapes=[
            pltpu.VMEM((BLOCKS, HEADS, OWN, DH), bf16),
            pltpu.VMEM((BLOCKS, DH, DH), bf16),
            pltpu.VMEM((BLOCKS, DH, DH), bf16),
            pltpu.VMEM((BLOCKS, 2, 3, DH, HALF), bf16),
            pltpu.VMEM((BLOCKS, 3, DH, HALF), bf16),
            pltpu.VMEM((BLOCKS, 3, CHIPS, OWN, HALF), bf16),
            pltpu.VMEM((BLOCKS, 3, others, OWN, HALF), bf16),
            pltpu.VMEM((BLOCKS, 3, 2, CHIPS, OWN, HALF), bf16),
            pltpu.VMEM((3, DH, FH), f32),
            pltpu.VMEM((3, DH, FH), bf16),
            pltpu.VMEM((BLOCKS, HEADS, OWN, DH), bf16),
            dma((8,)),
            dma((BLOCKS, 3)),
            dma((BLOCKS, 3)),
            dma((BLOCKS, 3)),
            dma((BLOCKS, 3)),
            dma((BLOCKS, 3)),
            dma((BLOCKS, 3, others)),
            dma((BLOCKS, 3)),
            dma((BLOCKS, 3)),
            dma((BLOCKS,)),
            dma((BLOCKS,)),
            pltpu.SemaphoreType.REGULAR((len(RING),)),
        ],
        compiler_params=pltpu.CompilerParams(
            collective_id=0, has_side_effects=True, vmem_limit_bytes=50_000_000
        ),
        name="ttt",
    )(learn_rates, *[pltpu.with_memory_space_constraint(array, pltpu.HBM) for array in arrays])


def solution(mesh):
    return jax.shard_map(
        on_device,
        mesh=mesh,
        in_specs=(
            P(None, "ctx", "head"),
            P(None, "ctx", "head"),
            P(None, "ctx", "head"),
            P("head", None, None),
            P("head", None, None),
            P("head", None, None),
            P("head"),
        ),
        out_specs=P(None, ("ctx", "head"), None),
        check_vma=False,
    )
```

```python
import jax
import jax.numpy as jnp
from jax import lax
from jax.experimental import pallas as pl
from jax.experimental.pallas import tpu as pltpu
from jax.sharding import PartitionSpec as P

BLOCKS = 2
NS_ITERS = 3
COEF_A = 3.4445
COEF_B = -4.775
COEF_C = 2.0315
EPSILON = 1e-06

SIDE = 4
CHIPS = SIDE * SIDE
HEADS = 16
DH = 256
FH = 512
HALF = 256
OWN = DH // CHIPS
MESH = pl.DeviceIdType.MESH

STEPS = sorted(
    [(dx, dy) for dx in range(SIDE) for dy in range(SIDE) if (dx, dy) != (0, 0)],
    key=lambda s: -(min(s[0], SIDE - s[0]) + min(s[1], SIDE - s[1])),
)
RING = (1, 2, 4)
ORDER = (2, 1, 0)
PARTS = 2
HOPS = sorted(range(1, HEADS), key=lambda o: -min(o, HEADS - o))


def nn(a, b):
    return jnp.dot(a, b, preferred_element_type=jnp.float32)


def nt(a, b):
    return lax.dot_general(a, b, (((1,), (1,)), ((), ())), preferred_element_type=jnp.float32)


def kernel(
    lr_ref,
    q_hbm,
    k_hbm,
    v_hbm,
    wg_hbm,
    wu_hbm,
    wd_hbm,
    out_ref,
    q_ref,
    k_ref,
    v_ref,
    mine,
    theirs,
    pairs,
    shares,
    whole,
    master,
    fast,
    made,
    load_s,
    pair_s,
    pair_r,
    share_s,
    share_r,
    whole_s,
    whole_r,
    twin_s,
    twin_r,
    out_s,
    out_r,
    ring,
):
    bf16, f32 = jnp.bfloat16, jnp.float32
    head = lax.axis_index("head")
    ctx = lax.axis_index("ctx")
    core = ctx % 2
    chip = ctx // 2
    x, y = chip // SIDE, chip % SIDE
    twin = {"ctx": ctx + 1 - 2 * core}

    def to_chip(step, sign=1):
        return (x + sign * step[0] + SIDE) % SIDE * SIDE + (y + sign * step[1] + SIDE) % SIDE

    def on_chip(other):
        return {"ctx": other * 2 + core}

    def send(src, dst, s, r, device):
        return pltpu.make_async_remote_copy(
            src_ref=src,
            dst_ref=dst,
            send_sem=s,
            recv_sem=r,
            device_id=device,
            device_id_type=MESH,
        )

    def load(i, src, dst):
        return pltpu.make_async_copy(src, dst, load_s.at[i])

    first = [
        load(0, k_hbm.at[0], k_ref.at[0]),
        load(1, wg_hbm.at[0], fast.at[0]),
        load(2, wu_hbm.at[0], fast.at[1]),
        load(3, v_hbm.at[0], v_ref.at[0]),
        load(4, wd_hbm.at[0], fast.at[2]),
    ]
    second = [load(5, k_hbm.at[1], k_ref.at[1]), load(6, v_hbm.at[1], v_ref.at[1])]
    for copy in first:
        copy.start()

    barrier = pltpu.get_barrier_semaphore()
    for z in (1, HEADS - 1):
        pl.semaphore_signal(
            barrier, inc=1, device_id={"head": (head + z) % HEADS}, device_id_type=MESH
        )
    for step in STEPS:
        pl.semaphore_signal(
            barrier, inc=1, device_id=on_chip(to_chip(step)), device_id_type=MESH
        )
    pl.semaphore_signal(barrier, inc=1, device_id=twin, device_id_type=MESH)

    def ring_signal(level):
        for z in (RING[level], HEADS - RING[level]):
            pl.semaphore_signal(
                ring.at[level], inc=1, device_id={"head": (head + z) % HEADS}, device_id_type=MESH
            )

    def ring_wait(level):
        pl.semaphore_wait(ring.at[level], 2)

    def load_queries():
        for b in range(BLOCKS):
            for i, o in enumerate(HOPS + [0]):
                rows = pl.ds(pl.multiple_of((head + o) % HEADS * OWN, OWN), OWN)
                load(7, q_hbm.at[b, rows], q_ref.at[b, i]).start()

    def pair_copy(b, m):
        return send(
            mine.at[b, 1 - core, m], theirs.at[b, m], pair_s.at[b, m], pair_r.at[b, m], twin
        )

    def share_copy(b, m, i):
        other = to_chip(STEPS[i])
        return send(
            pairs.at[b, m, other],
            shares.at[b, m, i],
            share_s.at[b, m],
            share_r.at[b, m],
            on_chip(other),
        )

    def all_shares(b, m):
        block = shares.at[b, m]
        return send(block, block, share_s.at[b, m], share_r.at[b, m], twin)

    def whole_copy(b, m, i):
        here = whole.at[b, m, core, chip]
        return send(
            here, here, whole_s.at[b, m], whole_r.at[b, m, i], on_chip(to_chip(STEPS[i]))
        )

    def all_wholes(b, m):
        block = shares.at[b, m]
        return send(block, block, whole_s.at[b, m], whole_r.at[b, m, 0], twin)

    def twin_copy(b, m, slot):
        here = whole.at[b, m, core, slot]
        return send(here, here, twin_s.at[b, m], twin_r.at[b, m], twin)

    def all_twins(b, m):
        block = whole.at[b, m, 1 - core]
        return send(block, block, twin_s.at[b, m], twin_r.at[b, m], twin)

    columns = pl.ds(pl.multiple_of(head * DH, DH), DH)

    def out_copy(b, i):
        return send(
            made.at[b, i],
            out_ref.at[b, :, columns],
            out_s.at[b],
            out_r.at[b],
            {"head": (head + HOPS[i]) % HEADS},
        )

    def all_outs(b):
        block = made.at[b, pl.ds(0, len(HOPS))]
        return send(block, block, out_s.at[b], out_r.at[b], twin)

    def gradients(b):
        def hand_over(m, rows_t, d):
            for j in range(2):
                mine[b, j, m] = nn(rows_t, d[:, j * HALF : (j + 1) * HALF]).astype(bf16)

        if b == 0:
            for copy in first[:3]:
                copy.wait()
        else:
            for copy in second:
                copy.wait()
        keys = k_ref[b]
        gate = nn(keys, fast[0])
        up = nn(keys, fast[1])
        sig = jax.nn.sigmoid(gate)
        act = gate * sig
        gated = (act * up).astype(bf16)
        if b == 0:
            for copy in first[3:]:
                copy.wait()
        values = v_ref[b]
        hand_over(2, values.T, gated)
        if b == 0:
            pl.semaphore_wait(barrier, len(STEPS) + 3)
            ring_signal(0)
        pair_copy(b, 2).start()
        back = nn(values, fast[2])
        keys_t = keys.T
        hand_over(1, keys_t, (back * act).astype(bf16))
        pair_copy(b, 1).start()
        d_gate = (back * up * sig * (1.0 + gate * (1.0 - sig))).astype(bf16)
        hand_over(0, keys_t, d_gate)
        pair_copy(b, 0).start()

    def start_shares(b):
        for m in ORDER:
            pair_copy(b, m).wait_recv()
            both = mine[b, core, m].astype(f32) + theirs[b, m].astype(f32)
            pairs[b, m] = both.astype(bf16).reshape(CHIPS, OWN, HALF)
            for i in range(len(STEPS)):
                share_copy(b, m, i).start()

    def start_wholes(b):
        for m in ORDER:
            all_shares(b, m).wait_recv()
            total = pairs[b, m, chip].astype(f32)
            for i in range(len(STEPS)):
                total = total + shares[b, m, i].astype(f32)
            whole[b, m, core, chip] = total.astype(bf16)
            twin_copy(b, m, chip).start()
            for i in range(len(STEPS)):
                whole_copy(b, m, i).start()

    def forward(b, m):
        for i in reversed(range(len(STEPS))):
            whole_copy(b, m, i).wait_recv()
            twin_copy(b, m, to_chip(STEPS[i], -1)).start()

    def finish_wholes(b):
        forward(b, 2)
        forward(b, 1)
        all_twins(b, 2).wait_recv()
        update(b, (2,), lambda: forward(b, 0))
        all_twins(b, 1).wait_recv()
        all_twins(b, 0).wait_recv()
        update(b, (0, 1))

    def update(b, which, between=None):
        now_b = [
            jnp.concatenate([whole[b, m, j].reshape(DH, HALF) for j in range(2)], axis=1)
            for m in which
        ]
        now = [g.astype(f32) for g in now_b]
        sizes = [jnp.sum(g * g, keepdims=True) for g in now]
        scales = [1.0 / (jnp.sqrt(size) + EPSILON) for size in sizes]
        for turn in range(NS_ITERS):
            grams = [nt(g, g) for g in now_b]
            if turn == 0:
                grams = [g * s * s for g, s in zip(grams, scales)]
            grams_b = [g.astype(bf16) for g in grams]
            polys = [COEF_B * g + COEF_C * nn(h, h) for g, h in zip(grams, grams_b)]
            now = [
                COEF_A * g + nn(poly.astype(bf16), h) for g, poly, h in zip(now, polys, now_b)
            ]
            if turn == 1 and between is not None:
                between()
            if turn == 0:
                now = [g * s for g, s in zip(now, scales)]
            now_b = [g.astype(bf16) for g in now]
        for m, step in zip(which, now):
            before = fast[m].astype(f32) if b == 0 else master[m]
            moved = before + lr_ref[0] * step
            if b + 1 < BLOCKS:
                master[m] = moved
            fast[m] = moved.astype(bf16)

    def answer(b):
        for part in range(PARTS):
            size = HEADS // PARTS
            rows = q_ref[b, part * size : (part + 1) * size].reshape(size * OWN, DH)
            gate = nn(rows, fast[0])
            up = nn(rows, fast[1])
            gated = (gate * jax.nn.sigmoid(gate) * up).astype(bf16)
            results = nt(gated, fast[2]).astype(bf16)
            made[b, part * size : (part + 1) * size] = results.reshape(size, OWN, DH)
            for i in range(part * size, min((part + 1) * size, len(HOPS))):
                out_copy(b, i).start()
        out_ref[b, :, columns] = made[b, len(HOPS)]

    gradients(0)
    start_shares(0)
    for copy in second:
        copy.start()
    load_queries()
    ring_wait(0)
    ring_signal(1)
    start_wholes(0)
    ring_wait(1)
    ring_signal(2)
    finish_wholes(0)
    gradients(1)
    start_shares(1)
    ring_wait(2)
    load(7, q_ref, q_ref).wait()
    answer(0)
    start_wholes(1)
    finish_wholes(1)
    answer(1)
    for b in range(BLOCKS):
        for m in ORDER:
            pair_copy(b, m).wait_send()
            all_shares(b, m).wait_send()
            all_wholes(b, m).wait_send()
            all_twins(b, m).wait_send()
        all_outs(b).wait()


def on_device(*operands):
    *arrays, learn_rates = operands
    bf16, f32 = jnp.bfloat16, jnp.float32
    others = len(STEPS)
    vmem = pl.BlockSpec(memory_space=pltpu.VMEM)
    hbm = pl.BlockSpec(memory_space=pltpu.HBM)
    dma = pltpu.SemaphoreType.DMA
    return pl.pallas_call(
        kernel,
        out_shape=jax.ShapeDtypeStruct((BLOCKS, OWN, HEADS * DH), bf16),
        in_specs=[pl.BlockSpec(memory_space=pltpu.SMEM)] + [hbm] * 6,
        out_specs=vmem,
        scratch_shapes=[
            pltpu.VMEM((BLOCKS, HEADS, OWN, DH), bf16),
            pltpu.VMEM((BLOCKS, DH, DH), bf16),
            pltpu.VMEM((BLOCKS, DH, DH), bf16),
            pltpu.VMEM((BLOCKS, 2, 3, DH, HALF), bf16),
            pltpu.VMEM((BLOCKS, 3, DH, HALF), bf16),
            pltpu.VMEM((BLOCKS, 3, CHIPS, OWN, HALF), bf16),
            pltpu.VMEM((BLOCKS, 3, others, OWN, HALF), bf16),
            pltpu.VMEM((BLOCKS, 3, 2, CHIPS, OWN, HALF), bf16),
            pltpu.VMEM((3, DH, FH), f32),
            pltpu.VMEM((3, DH, FH), bf16),
            pltpu.VMEM((BLOCKS, HEADS, OWN, DH), bf16),
            dma((8,)),
            dma((BLOCKS, 3)),
            dma((BLOCKS, 3)),
            dma((BLOCKS, 3)),
            dma((BLOCKS, 3)),
            dma((BLOCKS, 3)),
            dma((BLOCKS, 3, others)),
            dma((BLOCKS, 3)),
            dma((BLOCKS, 3)),
            dma((BLOCKS,)),
            dma((BLOCKS,)),
            pltpu.SemaphoreType.REGULAR((len(RING),)),
        ],
        compiler_params=pltpu.CompilerParams(
            collective_id=0, has_side_effects=True, vmem_limit_bytes=50_000_000
        ),
        name="ttt",
    )(learn_rates, *[pltpu.with_memory_space_constraint(array, pltpu.HBM) for array in arrays])


def solution(mesh):
    return jax.shard_map(
        on_device,
        mesh=mesh,
        in_specs=(
            P(None, "ctx", "head"),
            P(None, "ctx", "head"),
            P(None, "ctx", "head"),
            P("head", None, None),
            P("head", None, None),
            P("head", None, None),
            P("head"),
        ),
        out_specs=P(None, ("ctx", "head"), None),
        check_vma=False,
    )
```

```python
import jax
import jax.numpy as jnp
from jax import lax
from jax.experimental import pallas as pl
from jax.experimental.pallas import tpu as pltpu
from jax.sharding import PartitionSpec as P

BLOCKS = 2
NS_ITERS = 3
COEF_A = 3.4445
COEF_B = -4.775
COEF_C = 2.0315
EPSILON = 1e-06

SIDE = 4
CHIPS = SIDE * SIDE
HEADS = 16
DH = 256
FH = 512
HALF = 256
OWN = DH // CHIPS
MESH = pl.DeviceIdType.MESH

STEPS = sorted(
    [(dx, dy) for dx in range(SIDE) for dy in range(SIDE) if (dx, dy) != (0, 0)],
    key=lambda s: -(min(s[0], SIDE - s[0]) + min(s[1], SIDE - s[1])),
)
RING = (1, 2, 4)
ORDER = (2, 1, 0)
PARTS = 2
HOPS = sorted(range(1, HEADS), key=lambda o: -min(o, HEADS - o))


def nn(a, b):
    return jnp.dot(a, b, preferred_element_type=jnp.float32)


def nt(a, b):
    return lax.dot_general(a, b, (((1,), (1,)), ((), ())), preferred_element_type=jnp.float32)


def kernel(
    lr_ref,
    q_hbm,
    k_hbm,
    v_hbm,
    wg_hbm,
    wu_hbm,
    wd_hbm,
    out_ref,
    q_ref,
    k_ref,
    v_ref,
    mine,
    theirs,
    pairs,
    shares,
    whole,
    master,
    fast,
    made,
    turned,
    back_ref,
    load_s,
    pair_s,
    pair_r,
    share_s,
    share_r,
    whole_s,
    whole_r,
    twin_s,
    twin_r,
    out_s,
    out_r,
    ring,
):
    bf16, f32 = jnp.bfloat16, jnp.float32
    head = lax.axis_index("head")
    ctx = lax.axis_index("ctx")
    core = ctx % 2
    chip = ctx // 2
    x, y = chip // SIDE, chip % SIDE
    twin = {"ctx": ctx + 1 - 2 * core}

    def to_chip(step, sign=1):
        return (x + sign * step[0] + SIDE) % SIDE * SIDE + (y + sign * step[1] + SIDE) % SIDE

    def on_chip(other):
        return {"ctx": other * 2 + core}

    def send(src, dst, s, r, device):
        return pltpu.make_async_remote_copy(
            src_ref=src,
            dst_ref=dst,
            send_sem=s,
            recv_sem=r,
            device_id=device,
            device_id_type=MESH,
        )

    def load(i, src, dst):
        return pltpu.make_async_copy(src, dst, load_s.at[i])

    first = [
        load(0, k_hbm.at[0], k_ref.at[0]),
        load(1, wg_hbm.at[0], fast.at[0]),
        load(2, wu_hbm.at[0], fast.at[1]),
        load(3, v_hbm.at[0], v_ref.at[0]),
        load(4, wd_hbm.at[0], fast.at[2]),
    ]
    second = [load(5, k_hbm.at[1], k_ref.at[1]), load(6, v_hbm.at[1], v_ref.at[1])]
    for copy in first:
        copy.start()

    barrier = pltpu.get_barrier_semaphore()
    for z in (1, HEADS - 1):
        pl.semaphore_signal(
            barrier, inc=1, device_id={"head": (head + z) % HEADS}, device_id_type=MESH
        )
    for step in STEPS:
        pl.semaphore_signal(
            barrier, inc=1, device_id=on_chip(to_chip(step)), device_id_type=MESH
        )
    pl.semaphore_signal(barrier, inc=1, device_id=twin, device_id_type=MESH)

    def ring_signal(level):
        for z in (RING[level], HEADS - RING[level]):
            pl.semaphore_signal(
                ring.at[level], inc=1, device_id={"head": (head + z) % HEADS}, device_id_type=MESH
            )

    def ring_wait(level):
        pl.semaphore_wait(ring.at[level], 2)

    def load_queries():
        for b in range(BLOCKS):
            for i, o in enumerate(HOPS + [0]):
                rows = pl.ds(pl.multiple_of((head + o) % HEADS * OWN, OWN), OWN)
                load(7, q_hbm.at[b, rows], q_ref.at[b, i]).start()

    def pair_copy(b, m):
        return send(
            mine.at[b, 1 - core, m], theirs.at[b, m], pair_s.at[b, m], pair_r.at[b, m], twin
        )

    def share_copy(b, m, i):
        other = to_chip(STEPS[i])
        return send(
            pairs.at[b, m, other],
            shares.at[b, m, i],
            share_s.at[b, m],
            share_r.at[b, m],
            on_chip(other),
        )

    def all_shares(b, m):
        block = shares.at[b, m]
        return send(block, block, share_s.at[b, m], share_r.at[b, m], twin)

    def whole_copy(b, m, i):
        here = whole.at[b, m, core, chip]
        return send(
            here, here, whole_s.at[b, m], whole_r.at[b, m, i], on_chip(to_chip(STEPS[i]))
        )

    def all_wholes(b, m):
        block = shares.at[b, m]
        return send(block, block, whole_s.at[b, m], whole_r.at[b, m, 0], twin)

    def twin_copy(b, m, slot):
        here = whole.at[b, m, core, slot]
        return send(here, here, twin_s.at[b, m], twin_r.at[b, m], twin)

    def all_twins(b, m):
        block = whole.at[b, m, 1 - core]
        return send(block, block, twin_s.at[b, m], twin_r.at[b, m], twin)

    columns = pl.ds(pl.multiple_of(head * DH, DH), DH)

    def out_copy(b, i):
        return send(
            made.at[b, i],
            out_ref.at[b, :, columns],
            out_s.at[b],
            out_r.at[b],
            {"head": (head + HOPS[i]) % HEADS},
        )

    def all_outs(b):
        block = made.at[b, pl.ds(0, len(HOPS))]
        return send(block, block, out_s.at[b], out_r.at[b], twin)

    def gradients(b):
        def hand_over(m, rows_t, d):
            for j in range(2):
                mine[b, j, m] = nn(rows_t, d[:, j * HALF : (j + 1) * HALF]).astype(bf16)

        if b == 0:
            for copy in first[:3]:
                copy.wait()
        keys = k_ref[b]
        gate = nn(keys, fast[0])
        up = nn(keys, fast[1])
        sig = jax.nn.sigmoid(gate)
        act = gate * sig
        gated = (act * up).astype(bf16)
        if b == 0:
            for copy in first[3:]:
                copy.wait()
        values = v_ref[b]
        hand_over(2, values.T if b == 0 else turned[1], gated)
        if b == 0:
            pl.semaphore_wait(barrier, len(STEPS) + 3)
            ring_signal(0)
        pair_copy(b, 2).start()
        back = nn(values, fast[2]) if b == 0 else back_ref[...]
        keys_t = keys.T if b == 0 else turned[0]
        hand_over(1, keys_t, (back * act).astype(bf16))
        pair_copy(b, 1).start()
        d_gate = (back * up * sig * (1.0 + gate * (1.0 - sig))).astype(bf16)
        hand_over(0, keys_t, d_gate)
        pair_copy(b, 0).start()

    def start_shares(b):
        for m in ORDER:
            pair_copy(b, m).wait_recv()
            both = mine[b, core, m].astype(f32) + theirs[b, m].astype(f32)
            pairs[b, m] = both.astype(bf16).reshape(CHIPS, OWN, HALF)
            for i in range(len(STEPS)):
                share_copy(b, m, i).start()

    def start_wholes(b):
        for m in ORDER:
            all_shares(b, m).wait_recv()
            total = pairs[b, m, chip].astype(f32)
            for i in range(len(STEPS)):
                total = total + shares[b, m, i].astype(f32)
            whole[b, m, core, chip] = total.astype(bf16)
            twin_copy(b, m, chip).start()
            for i in range(len(STEPS)):
                whole_copy(b, m, i).start()

    def forward(b, m):
        for i in reversed(range(len(STEPS))):
            whole_copy(b, m, i).wait_recv()
            twin_copy(b, m, to_chip(STEPS[i], -1)).start()

    def finish_wholes(b):
        forward(b, 2)
        forward(b, 1)
        all_twins(b, 2).wait_recv()
        update(b, (2,), lambda: forward(b, 0))
        if b + 1 < BLOCKS:
            back_ref[...] = nn(v_ref[b + 1], fast[2])
        all_twins(b, 1).wait_recv()
        all_twins(b, 0).wait_recv()
        update(b, (0, 1))

    def update(b, which, between=None):
        now_b = [
            jnp.concatenate([whole[b, m, j].reshape(DH, HALF) for j in range(2)], axis=1)
            for m in which
        ]
        now = [g.astype(f32) for g in now_b]
        sizes = [jnp.sum(g * g, keepdims=True) for g in now]
        scales = [1.0 / (jnp.sqrt(size) + EPSILON) for size in sizes]
        for turn in range(NS_ITERS):
            grams = [nt(g, g) for g in now_b]
            if turn == 0:
                grams = [g * s * s for g, s in zip(grams, scales)]
            grams_b = [g.astype(bf16) for g in grams]
            polys = [COEF_B * g + COEF_C * nn(h, h) for g, h in zip(grams, grams_b)]
            now = [
                COEF_A * g + nn(poly.astype(bf16), h) for g, poly, h in zip(now, polys, now_b)
            ]
            if turn == 1 and between is not None:
                between()
            if turn == 0:
                now = [g * s for g, s in zip(now, scales)]
            now_b = [g.astype(bf16) for g in now]
        for m, step in zip(which, now):
            before = fast[m].astype(f32) if b == 0 else master[m]
            moved = before + lr_ref[0] * step
            if b + 1 < BLOCKS:
                master[m] = moved
            fast[m] = moved.astype(bf16)

    def answer(b):
        for part in range(PARTS):
            size = HEADS // PARTS
            rows = q_ref[b, part * size : (part + 1) * size].reshape(size * OWN, DH)
            gate = nn(rows, fast[0])
            up = nn(rows, fast[1])
            gated = (gate * jax.nn.sigmoid(gate) * up).astype(bf16)
            results = nt(gated, fast[2]).astype(bf16)
            made[b, part * size : (part + 1) * size] = results.reshape(size, OWN, DH)
            for i in range(part * size, min((part + 1) * size, len(HOPS))):
                out_copy(b, i).start()
        out_ref[b, :, columns] = made[b, len(HOPS)]

    gradients(0)
    start_shares(0)
    for copy in second:
        copy.start()
    load_queries()
    ring_wait(0)
    ring_signal(1)
    start_wholes(0)
    ring_wait(1)
    ring_signal(2)
    for copy in second:
        copy.wait()
    turned[0] = k_ref[1].T
    turned[1] = v_ref[1].T
    finish_wholes(0)
    gradients(1)
    start_shares(1)
    ring_wait(2)
    load(7, q_ref, q_ref).wait()
    answer(0)
    start_wholes(1)
    finish_wholes(1)
    answer(1)
    for b in range(BLOCKS):
        for m in ORDER:
            pair_copy(b, m).wait_send()
            all_shares(b, m).wait_send()
            all_wholes(b, m).wait_send()
            all_twins(b, m).wait_send()
        all_outs(b).wait()


def on_device(*operands):
    *arrays, learn_rates = operands
    bf16, f32 = jnp.bfloat16, jnp.float32
    others = len(STEPS)
    vmem = pl.BlockSpec(memory_space=pltpu.VMEM)
    hbm = pl.BlockSpec(memory_space=pltpu.HBM)
    dma = pltpu.SemaphoreType.DMA
    return pl.pallas_call(
        kernel,
        out_shape=jax.ShapeDtypeStruct((BLOCKS, OWN, HEADS * DH), bf16),
        in_specs=[pl.BlockSpec(memory_space=pltpu.SMEM)] + [hbm] * 6,
        out_specs=vmem,
        scratch_shapes=[
            pltpu.VMEM((BLOCKS, HEADS, OWN, DH), bf16),
            pltpu.VMEM((BLOCKS, DH, DH), bf16),
            pltpu.VMEM((BLOCKS, DH, DH), bf16),
            pltpu.VMEM((BLOCKS, 2, 3, DH, HALF), bf16),
            pltpu.VMEM((BLOCKS, 3, DH, HALF), bf16),
            pltpu.VMEM((BLOCKS, 3, CHIPS, OWN, HALF), bf16),
            pltpu.VMEM((BLOCKS, 3, others, OWN, HALF), bf16),
            pltpu.VMEM((BLOCKS, 3, 2, CHIPS, OWN, HALF), bf16),
            pltpu.VMEM((3, DH, FH), f32),
            pltpu.VMEM((3, DH, FH), bf16),
            pltpu.VMEM((BLOCKS, HEADS, OWN, DH), bf16),
            pltpu.VMEM((2, DH, DH), bf16),
            pltpu.VMEM((DH, FH), f32),
            dma((8,)),
            dma((BLOCKS, 3)),
            dma((BLOCKS, 3)),
            dma((BLOCKS, 3)),
            dma((BLOCKS, 3)),
            dma((BLOCKS, 3)),
            dma((BLOCKS, 3, others)),
            dma((BLOCKS, 3)),
            dma((BLOCKS, 3)),
            dma((BLOCKS,)),
            dma((BLOCKS,)),
            pltpu.SemaphoreType.REGULAR((len(RING),)),
        ],
        compiler_params=pltpu.CompilerParams(
            collective_id=0, has_side_effects=True, vmem_limit_bytes=50_000_000
        ),
        name="ttt",
    )(learn_rates, *[pltpu.with_memory_space_constraint(array, pltpu.HBM) for array in arrays])


def solution(mesh):
    return jax.shard_map(
        on_device,
        mesh=mesh,
        in_specs=(
            P(None, "ctx", "head"),
            P(None, "ctx", "head"),
            P(None, "ctx", "head"),
            P("head", None, None),
            P("head", None, None),
            P("head", None, None),
            P("head"),
        ),
        out_specs=P(None, ("ctx", "head"), None),
        check_vma=False,
    )
```
